256 devices in a mesh: dp: 8 (over y, core), expert: 32 (over x, z).
Axes of the slice: x: 4, y: 4, z: 8, core: 2. Of those that a mesh axis runs over, the one named last changes fastest.
Arguments:
- tokens: bfloat16 [32768, 5120], P(('dp', 'expert')), may hold values from -6 to 6
- grad_out: bfloat16 [32768, 5120], P(('dp', 'expert')), may hold values from -1.5 to 1.5
- expert_ids: int32 [32768, 2], P(('dp', 'expert')), may hold values from 0 to 31, as said below
- gate_codes: int32 [32768, 2], P(('dp', 'expert')), may hold values from 1 to 1023
- w_up: bfloat16 [32, 5120, 768], P('expert', 'dp'), may hold values from -0.078125 to 0.078125
- w_down: bfloat16 [32, 5120, 768], P('expert', 'dp'), may hold values from -2.5 to 2.5
Outputs:
- layer_output: bfloat16 [32768, 5120], P(('dp', 'expert'))
- grad_tokens: bfloat16 [32768, 5120], P(('dp', 'expert'))
- grad_up: bfloat16 [32, 5120, 768], P('expert', 'dp')
- grad_down: bfloat16 [32, 5120, 768], P('expert', 'dp')
The draws below stay inside these ranges and needn't reach their ends.
Inputs may be any that keep to these rules, and one draw needn't show every extreme that they name: `expert_ids`: each row names two different experts. Among the rows of one device no expert is named more than 9 times, and in every draw one expert is named exactly 9 times by the rows of every device.
All inputs are finite; a program needn't handle non-finite values.
Results may differ from the reference program's by a relative error of at most 0.0065.
Values may be sent and summed in bfloat16 or wider, within the bound.
A program may use at most 192 MiB of HBM per device.

```python
import math
import jax
import jax.numpy as jnp
from jax import lax

D = 5120
H = 768
LAYERS = 40
TOK_DEV = 128
EXPERTS = 32
TOKENS = 32768
CAP = 9
N_DP = 8
N_EXPERT = 32


def draw_expert_ids(key, part):
    block_count = TOKENS // TOK_DEV
    hot_expert = jax.random.randint(jax.random.fold_in(key, 7), (), 0, EXPERTS).astype(jnp.int32)
    unit_count = (EXPERTS - 1) * CAP
    drop_count = EXPERTS * CAP - 2 * TOK_DEV
    kept_total = 2 * TOK_DEV - CAP

    def one_block(block_index):
        block_key = jax.random.fold_in(key, block_index)
        unit_ranks = jax.random.permutation(jax.random.fold_in(block_key, 1), unit_count)
        kept = unit_ranks >= drop_count
        chosen = jnp.nonzero(kept, size=kept_total, fill_value=0)[0].astype(jnp.int32)
        others = (chosen // CAP).astype(jnp.int32)
        others = others + (others >= hot_expert).astype(jnp.int32)
        entries = jnp.concatenate([jnp.full((CAP,), 1, jnp.int32) * hot_expert, others])
        paired = jnp.stack([entries[:TOK_DEV], entries[TOK_DEV:]], axis=1)
        row_order = jax.random.permutation(jax.random.fold_in(block_key, 2), TOK_DEV)
        return paired[row_order]
    return jax.vmap(one_block)(jnp.arange(block_count, dtype=jnp.int32)).reshape(TOKENS, 2)


def set_ends(values, stream_key, smallest, high):
    longest = values.shape.index(max(values.shape))
    spots = []
    for shift in (0, 1):
        where = [jax.random.randint(jax.random.fold_in(stream_key, axis), (), 0, length) for axis, length in enumerate(values.shape)]
        where[longest] = (where[longest] + shift) % values.shape[longest]
        spots.append(tuple(where))
    return values.at[spots[0]].set(smallest).at[spots[1]].set(high)


def steps_of(stream_key, shape, cuts, smallest, top_value):
    def one(dim, blocks):
        draws = jax.random.uniform(jax.random.fold_in(jax.random.fold_in(stream_key, 6), dim), (blocks,), jnp.float32, smallest / len(cuts), top_value / len(cuts))
        return jnp.repeat(jnp.exp(draws), shape[dim] // blocks).reshape((-1,) + (1,) * (len(shape) - dim - 1))

    level = one(*cuts[0])
    for cut in cuts[1:]:
        level = level * one(*cut)
    return level


def noise(rng, extent, width, bound, split=(), kind=jnp.bfloat16):
    drawn = width * jax.random.normal(rng, extent, jnp.float32)
    if split:
        drawn = drawn * steps_of(rng, extent, split, -0.22, 0.18)
    return jnp.clip(drawn, -bound, bound).astype(kind)


def setup_inputs(seed: int = 0) -> dict:
    splits = jax.random.split(jax.random.key(seed), 7)
    tokens = noise(splits[0], (TOKENS, D), 1.0, 6.0, ((0, 256),))
    grad_out = noise(splits[1], (TOKENS, D), 0.25, 1.5, ((0, 256),))
    expert_ids = draw_expert_ids(jax.random.fold_in(splits[6], 71), 0)
    gate_codes = set_ends(jax.random.randint(splits[3], (TOKENS, 2), 1, 1024), jax.random.fold_in(splits[3], 1), 1, 1023).astype(jnp.int32)
    w_up = noise(splits[4], (EXPERTS, D, H), D ** -0.5, 0.078125, ((0, 32), (1, 8)))
    w_down = noise(splits[5], (EXPERTS, D, H), (max(1, H // 128)) ** -0.5, 2.5, ((0, 32), (1, 8)))
    return dict(tokens=tokens, grad_out=grad_out, expert_ids=expert_ids, gate_codes=gate_codes, w_up=w_up, w_down=w_down)


def activate(values):
    return jax.nn.gelu(values, approximate=True)

def contract_rows(former, latter):
    return lax.dot_general(former, latter, (((0,), (0,)), ((), ())), preferred_element_type=jnp.float32)

def contract_columns(former, latter):
    return lax.dot_general(former, latter, (((1,), (1,)), ((), ())), preferred_element_type=jnp.float32)

def reference(tokens, grad_out, expert_ids, gate_codes, w_up, w_down):
    out_scale = 1.0 / math.sqrt(2.0 * LAYERS)
    gate_values = gate_codes.astype(jnp.float32)
    flat_gates = (gate_values / lax.optimization_barrier(jnp.sum(gate_values, axis=1, keepdims=True))).reshape(-1)
    flat_ids = expert_ids.reshape(-1)
    flat_rows = (jnp.arange(2 * TOKENS, dtype=jnp.int32) // 2).astype(jnp.int32)
    most_rows = N_DP * N_EXPERT * CAP

    def one_expert(running, inputs):
        mixed_sum, input_sum = running
        expert_index, up_weight, down_weight = inputs
        matches = flat_ids == expert_index
        picked = jnp.nonzero(matches, size=most_rows, fill_value=0)[0].astype(jnp.int32)
        live_slot = jnp.arange(most_rows, dtype=jnp.int32) < jnp.sum(matches.astype(jnp.int32))
        token_rows = flat_rows[picked]
        weights = jnp.where(live_slot, flat_gates[picked], jnp.zeros((), flat_gates.dtype))
        inputs_here = jnp.where(live_slot[:, None], tokens[token_rows], jnp.zeros((), tokens.dtype))
        slot_grads = (out_scale * weights[:, None] * grad_out[token_rows].astype(jnp.float32)).astype(jnp.bfloat16)
        pre_act = jnp.dot(inputs_here, up_weight, preferred_element_type=jnp.float32)
        hidden = activate(pre_act).astype(jnp.bfloat16)
        expert_out = contract_columns(hidden, down_weight).astype(jnp.bfloat16)
        hidden_grad = jnp.dot(slot_grads, down_weight, preferred_element_type=jnp.float32)
        pre_grad = jax.vjp(activate, pre_act)[1](hidden_grad)[0].astype(jnp.bfloat16)
        row_grad = contract_columns(pre_grad, up_weight).astype(jnp.bfloat16)
        up_grad = contract_rows(inputs_here, pre_grad).astype(jnp.bfloat16)
        down_grad = contract_rows(slot_grads, hidden).astype(jnp.bfloat16)
        mixed_sum = mixed_sum.at[token_rows].add(out_scale * weights[:, None] * expert_out.astype(jnp.float32))
        input_sum = input_sum.at[token_rows].add(row_grad.astype(jnp.float32))
        return ((mixed_sum, input_sum), (up_grad, down_grad))
    initial = (jnp.zeros((TOKENS, D), jnp.float32), jnp.zeros((TOKENS, D), jnp.float32))
    (mixed_sum, input_sum), (grad_up, grad_down) = lax.scan(one_expert, initial, (jnp.arange(EXPERTS, dtype=jnp.int32), w_up, w_down))
    return (mixed_sum.astype(jnp.bfloat16), input_sum.astype(jnp.bfloat16), grad_up, grad_down)
```

```python
import functools
import math

import jax
import jax.numpy as jnp
from jax import lax
from jax.experimental import pallas as pl
from jax.experimental.pallas import tpu as pltpu
from jax.sharding import PartitionSpec as P

LAYERS = 40
NX, NZ = 4, 8
NY, NCORE = 4, 2
NE, ND = NX * NZ, NY * NCORE
MESH = pl.DeviceIdType.MESH
F32, BF16, I32 = jnp.float32, jnp.bfloat16, jnp.int32
OUT_SCALE = 1.0 / math.sqrt(2.0 * LAYERS)
GELU_C = math.sqrt(2.0 / math.pi)


def iota(shape, dim):
    return lax.broadcasted_iota(I32, shape, dim)


def as_bf16(cond):
    return jnp.where(cond, 1.0, 0.0).astype(BF16)


def dot(a, b):
    return jnp.dot(a, b, preferred_element_type=F32)


def dot_cols(a, b):
    return lax.dot_general(a, b, (((1,), (1,)), ((), ())), preferred_element_type=F32)


def dot_rows(a, b):
    return lax.dot_general(a, b, (((0,), (0,)), ((), ())), preferred_element_type=F32)


def slots_in_lanes(ids):
    t = ids.shape[1]
    e0, e1 = ids[0:1, :], ids[1:2, :]
    experts = iota((NE, t), 0)
    oh0, oh1 = as_bf16(experts == e0), as_bf16(experts == e1)
    earlier = as_bf16(iota((t, t), 0) < iota((t, t), 1))
    c0 = dot(oh0, earlier)
    c1 = dot(oh1, earlier) + jnp.sum(oh0.astype(F32), axis=1, keepdims=True)
    b0 = jnp.sum(c0 * oh0.astype(F32), axis=0, keepdims=True).astype(I32)
    b1 = jnp.sum(c1 * oh1.astype(F32), axis=0, keepdims=True).astype(I32)
    return e0, e1, b0, b1


def slots_in_rows(ids):
    t = ids.shape[0]
    e0, e1 = ids[:, 0:1], ids[:, 1:2]
    experts = iota((t, 128), 1)
    oh0, oh1 = as_bf16(experts == e0), as_bf16(experts == e1)
    earlier = as_bf16(iota((t, t), 1) < iota((t, t), 0))
    c0 = dot(earlier, oh0)
    c1 = dot(earlier, oh1) + jnp.sum(oh0.astype(F32), axis=0, keepdims=True)
    b0 = jnp.sum(c0 * oh0.astype(F32), axis=1, keepdims=True).astype(I32)
    b1 = jnp.sum(c1 * oh1.astype(F32), axis=1, keepdims=True).astype(I32)
    return e0, e1, b0, b1


def gelu(v):
    return 0.5 * v * (1.0 + jnp.tanh(GELU_C * (v + 0.044715 * (v * v * v))))


def gelu_slope(v):
    th = jnp.tanh(GELU_C * (v + 0.044715 * (v * v * v)))
    return 0.5 * (1.0 + th) + 0.5 * v * (1.0 - th * th) * (GELU_C * (1.0 + 3.0 * 0.044715 * (v * v)))


def kernel(
    tok_ref, grad_ref, ids_ref, idst_ref, codes_ref, codest_ref, wup_hbm, wdown_hbm,
    out_ref, gtok_ref, gup_ref, gdown_ref,
    send_a, send_b, recv_a, recv_b, back_a, back_b, wup, wdown, xall, gall, hall, pall,
    acc, acc2, fold, wacc,
    a2a_send, a2a_recv, w_send, w_recv, p_send, p_recv, s_send, s_recv, h_send, h_recv, loc,
):
    T = tok_ref.shape[0]
    NS = NE * 8
    R = NS + NE
    CW = wup.shape[1]
    dp, me = lax.axis_index("dp"), lax.axis_index("expert")
    x, z = lax.div(me, NZ), lax.rem(me, NZ)
    y, core = lax.div(dp, NCORE), lax.rem(dp, NCORE)
    mate = y * NCORE + (1 - core)

    def peer(k):
        return lax.rem(x + lax.div(k, NZ), NX) * NZ + lax.rem(z + lax.rem(k, NZ), NZ)

    def dpeer(k):
        return lax.rem(dp + k, ND)

    def ypeer(k):
        return lax.rem(y + k, NY) * NCORE + core

    def each(lo, hi, body):
        def step(k, carry):
            body(k)
            return carry
        lax.fori_loop(lo, hi, step, 0)

    def a2a(wave, src, dst, k):
        t = peer(k)
        return pltpu.make_async_remote_copy(
            src_ref=src.at[:, pl.ds(pl.multiple_of(t * 8, 8), 8), :],
            dst_ref=dst.at[:, pl.ds(pl.multiple_of(me * 8, 8), 8), :],
            send_sem=a2a_send.at[wave * NE + k], recv_sem=a2a_recv.at[wave * NE + k],
            device_id={"expert": t}, device_id_type=MESH)

    def own(wave, src, dst):
        rows = pl.ds(pl.multiple_of(me * 8, 8), 8)
        return pltpu.make_async_copy(src.at[:, rows, :], dst.at[:, rows, :], loc.at[wave])

    def start_wave(wave, src, dst):
        own(wave, src, dst).start()
        each(1, NE, lambda k: a2a(wave, src, dst, k).start())

    def sent_wave(wave, src, dst):
        each(1, NE, lambda k: a2a(wave, src, dst, k).wait_send())

    def landed_wave(wave, src, dst):
        own(wave, src, dst).wait()
        each(1, NE, lambda k: a2a(wave, src, dst, k).wait_recv())

    def weight(i, k):
        src, dst = ((wup_hbm, wup), (wdown_hbm, wdown))[i]
        return pltpu.make_async_remote_copy(
            src_ref=src.at[0], dst_ref=dst.at[dp],
            send_sem=w_send.at[i * NY + k], recv_sem=w_recv.at[i * NY + k],
            device_id={"dp": ypeer(k)}, device_id_type=MESH)

    def weight_own(i):
        src, dst = ((wup_hbm, wup), (wdown_hbm, wdown))[i]
        return pltpu.make_async_copy(src.at[0], dst.at[dp], loc.at[4 + i])

    def weight_mate0(i):
        src, dst = ((wup_hbm, wup), (wdown_hbm, wdown))[i]
        return pltpu.make_async_remote_copy(
            src_ref=src.at[0], dst_ref=dst.at[dp],
            send_sem=p_send.at[i * NY], recv_sem=p_recv.at[i * NY],
            device_id={"dp": mate}, device_id_type=MESH)

    def weight_mate(i, k):
        buf = (wup, wdown)[i]
        j = lax.rem(y + NY - k, NY) * NCORE + core
        return pltpu.make_async_remote_copy(
            src_ref=buf.at[j], dst_ref=buf.at[j],
            send_sem=p_send.at[i * NY + k], recv_sem=p_recv.at[i * NY + k],
            device_id={"dp": mate}, device_id_type=MESH)

    def slices(i, k):
        src, dst = ((recv_a, xall), (recv_b, gall))[i]
        t = dpeer(k)
        return pltpu.make_async_remote_copy(
            src_ref=src.at[t], dst_ref=dst.at[dp],
            send_sem=s_send.at[i * ND + k], recv_sem=s_recv.at[i * ND + k],
            device_id={"dp": t}, device_id_type=MESH)

    def slice_own(i):
        src, dst = ((recv_a, xall), (recv_b, gall))[i]
        return pltpu.make_async_copy(src.at[dp], dst.at[dp], loc.at[6 + i])

    def acts(i, k):
        buf = (hall, pall)[i]
        return pltpu.make_async_remote_copy(
            src_ref=buf.at[dp], dst_ref=buf.at[dp],
            send_sem=h_send.at[i * ND + k], recv_sem=h_recv.at[i * ND + k],
            device_id={"dp": dpeer(k)}, device_id_type=MESH)

    barrier = pltpu.get_barrier_semaphore()
    each(1, NE, lambda k: pl.semaphore_signal(
        barrier, inc=1, device_id={"expert": peer(k)}, device_id_type=MESH))
    each(1, ND, lambda k: pl.semaphore_signal(
        barrier, inc=1, device_id={"dp": dpeer(k)}, device_id_type=MESH))
    weight_own(0).start()
    weight_own(1).start()

    e0, e1, b0, b1 = slots_in_lanes(idst_ref[...])
    s_iota = iota((NS, T), 0)
    s_exp, s_pos = lax.div(s_iota, 8), lax.rem(s_iota, 8)
    m0 = (s_iota == e0 * 8 + b0) & (b0 < 8)
    m1 = (s_iota == e1 * 8 + b1) & (b1 < 8)
    n0 = (s_exp == e0) & (b0 == 8)
    n1 = (s_exp == e1) & (b1 == 8)
    pick = as_bf16(m0 | m1)
    gv0, gv1 = codest_ref[0:1, :].astype(F32), codest_ref[1:2, :].astype(F32)
    gs = gv0 + gv1
    w0, w1 = OUT_SCALE * (gv0 / gs), OUT_SCALE * (gv1 / gs)
    zero = jnp.zeros((), F32)
    scale = jnp.sum(jnp.where(m0, w0, zero) + jnp.where(m1, w1, zero), axis=1, keepdims=True)
    scale9 = jnp.sum(jnp.where(n0, w0, zero) + jnp.where(n1, w1, zero), axis=1, keepdims=True)
    ninth = n0 | n1

    def cols(c):
        return pl.ds(pl.multiple_of(c * CW, 128), CW)

    def gather(src, dst, mul, mul9):
        fold[...] = jnp.zeros_like(fold)

        def body(c):
            part = src[:, cols(c)]
            rows = dot(pick, part)
            dst[c] = (rows if mul is None else rows * mul).astype(BF16)
            fold[...] += dot(as_bf16(ninth & (s_pos == c)), part)
        each(0, ND, body)
        dst[ND] = (fold[...] if mul9 is None else fold[...] * mul9).astype(BF16)

    gather(tok_ref, send_a, None, None)
    pl.semaphore_wait(barrier, NE - 1 + ND - 1)
    start_wave(0, send_a, recv_a)
    each(1, NY, lambda k: weight(0, k).start())
    weight_mate0(0).start()
    each(1, NY, lambda k: weight(1, k).start())
    weight_mate0(1).start()
    gather(grad_ref, send_b, scale, scale9)
    start_wave(1, send_b, recv_b)

    def pass_on(i):
        def body(k):
            weight(i, k).wait_recv()
            weight_mate(i, k).start()
        each(1, NY, body)

    pass_on(0)

    def unfold(buf):
        tail = buf[ND, 0:NS, :]

        def body(c):
            sel = as_bf16(iota((NE, NS), 1) == iota((NE, NS), 0) * 8 + c)
            buf[c, NS:R, :] = dot(sel, tail).astype(BF16)
        each(0, ND, body)

    landed_wave(0, send_a, recv_a)
    unfold(recv_a)
    slice_own(0).start()
    each(1, ND, lambda k: slices(0, k).start())

    weight_own(0).wait()
    weight_mate0(0).wait_recv()
    each(1, NY, lambda k: weight_mate(0, k).wait_recv())

    def contract(dst, rows, mat):
        dst[...] = jnp.zeros_like(dst)

        def body(c):
            dst[...] += dot(rows[c], mat[c])
        each(0, ND, body)

    contract(acc, recv_a, wup)
    hall[dp] = gelu(acc[...]).astype(BF16)
    each(1, ND, lambda k: acts(0, k).start())
    pass_on(1)
    weight_own(1).wait()
    weight_mate0(1).wait_recv()
    each(1, NY, lambda k: weight_mate(1, k).wait_recv())

    def expand(rows, mat, dst):
        fold[...] = jnp.zeros_like(fold)

        def body(c):
            o = dot_cols(rows, mat[c]).astype(BF16)
            dst[c] = o[0:NS]
            put = as_bf16(iota((NS, NE), 0) == iota((NS, NE), 1) * 8 + c)
            fold[...] += dot(put, o[NS:R])
        each(0, ND, body)
        dst[ND] = fold[...].astype(BF16)

    sent_wave(0, send_a, recv_a)
    expand(hall[dp], wdown, send_a)
    start_wave(2, send_a, back_a)

    landed_wave(1, send_b, recv_b)
    unfold(recv_b)
    slice_own(1).start()
    each(1, ND, lambda k: slices(1, k).start())
    contract(acc2, recv_b, wdown)
    pall[dp] = (acc2[...] * gelu_slope(acc[...])).astype(BF16)
    each(1, ND, lambda k: acts(1, k).start())
    sent_wave(1, send_b, recv_b)
    expand(pall[dp], wup, send_b)
    start_wave(3, send_b, back_b)

    def weight_grad(i, act, rows, dst):
        other = (hall, pall)[act]
        slice_own(i).wait()
        each(1, ND, lambda k: slices(i, k).wait_recv())
        each(1, ND, lambda k: acts(act, k).wait_recv())
        wacc[...] = jnp.zeros_like(wacc)

        def body(j):
            wacc[...] += dot_rows(rows[j], other[j])
        each(0, ND, body)
        dst[0] = wacc[...].astype(BF16)

    weight_grad(1, 0, gall, gdown_ref)
    weight_grad(0, 1, xall, gup_ref)

    f0, f1, r0, r1 = slots_in_rows(ids_ref[...])
    t_iota = iota((T, NS), 1)
    q0 = as_bf16((t_iota == f0 * 8 + r0) & (r0 < 8))
    q1 = as_bf16((t_iota == f1 * 8 + r1) & (r1 < 8))
    u0, u1 = codes_ref[:, 0:1].astype(F32), codes_ref[:, 1:2].astype(F32)
    us = u0 + u1
    v0, v1 = OUT_SCALE * (u0 / us), OUT_SCALE * (u1 / us)
    landed_wave(2, send_a, back_a)

    def mix(c):
        k0 = as_bf16((t_iota == f0 * 8 + c) & (r0 == 8))
        k1 = as_bf16((t_iota == f1 * 8 + c) & (r1 == 8))
        main, tail = back_a[c], back_a[ND]
        first = dot(q0, main) + dot(k0, tail)
        second = dot(q1, main) + dot(k1, tail)
        out_ref[:, cols(c)] = (first * v0 + second * v1).astype(BF16)
    each(0, ND, mix)

    qs = q0 + q1
    landed_wave(3, send_b, back_b)

    def mix_grad(c):
        ks = as_bf16(((t_iota == f0 * 8 + c) & (r0 == 8)) | ((t_iota == f1 * 8 + c) & (r1 == 8)))
        gtok_ref[:, cols(c)] = (dot(qs, back_b[c]) + dot(ks, back_b[ND])).astype(BF16)
    each(0, ND, mix_grad)

    sent_wave(2, send_a, back_a)
    sent_wave(3, send_b, back_b)
    for i in (0, 1):
        each(1, NY, lambda k: weight(i, k).wait_send())
        weight_mate0(i).wait_send()
        each(1, NY, lambda k: weight_mate(i, k).wait_send())
        each(1, ND, lambda k: slices(i, k).wait_send())
        each(1, ND, lambda k: acts(i, k).wait_send())


def local(tokens, grad_out, expert_ids, gate_codes, w_up, w_down):
    t, d = tokens.shape
    cw, h = w_up.shape[1], w_up.shape[2]
    ns, r = NE * 8, NE * 9
    vmem = pl.BlockSpec(memory_space=pltpu.VMEM)
    hbm = pl.BlockSpec(memory_space=pl.ANY)
    dma = pltpu.SemaphoreType.DMA
    return pl.pallas_call(
        kernel,
        name="moe",
        out_shape=(
            jax.ShapeDtypeStruct((t, d), BF16),
            jax.ShapeDtypeStruct((t, d), BF16),
            jax.ShapeDtypeStruct((1, cw, h), BF16),
            jax.ShapeDtypeStruct((1, cw, h), BF16),
        ),
        in_specs=[vmem] * 6 + [hbm] * 2,
        out_specs=(vmem,) * 4,
        scratch_shapes=[
            pltpu.VMEM((ND + 1, ns, cw), BF16), pltpu.VMEM((ND + 1, ns, cw), BF16),
            pltpu.VMEM((ND + 1, r, cw), BF16), pltpu.VMEM((ND + 1, r, cw), BF16),
            pltpu.VMEM((ND + 1, ns, cw), BF16), pltpu.VMEM((ND + 1, ns, cw), BF16),
            pltpu.VMEM((ND, cw, h), BF16), pltpu.VMEM((ND, cw, h), BF16),
            pltpu.VMEM((ND, r, cw), BF16), pltpu.VMEM((ND, r, cw), BF16),
            pltpu.VMEM((ND, r, h), BF16), pltpu.VMEM((ND, r, h), BF16),
            pltpu.VMEM((r, h), F32), pltpu.VMEM((r, h), F32),
            pltpu.VMEM((ns, cw), F32), pltpu.VMEM((cw, h), F32),
            dma((4 * NE,)), dma((4 * NE,)), dma((2 * NY,)), dma((2 * NY,)),
            dma((2 * NY,)), dma((2 * NY,)), dma((2 * ND,)), dma((2 * ND,)),
            dma((2 * ND,)), dma((2 * ND,)), dma((8,)),
        ],
        compiler_params=pltpu.CompilerParams(
            collective_id=0, has_side_effects=True, vmem_limit_bytes=67043328),
    )(tokens, grad_out, expert_ids, expert_ids.T, gate_codes, gate_codes.T, w_up, w_down)


def solution(mesh):
    rows = P(("dp", "expert"), None)
    shard = P("expert", "dp", None)
    return jax.shard_map(
        local, mesh=mesh, in_specs=(rows,) * 4 + (shard,) * 2,
        out_specs=(rows, rows, shard, shard), check_vma=False)
```

```python
import functools
import math

import jax
import jax.numpy as jnp
from jax import lax
from jax.experimental import pallas as pl
from jax.experimental.pallas import tpu as pltpu
from jax.sharding import PartitionSpec as P

LAYERS = 40
NX, NZ = 4, 8
NY, NCORE = 4, 2
NE, ND = NX * NZ, NY * NCORE
MESH = pl.DeviceIdType.MESH
F32, BF16, I32 = jnp.float32, jnp.bfloat16, jnp.int32
PARTS = (((0, 4), (4, 5)), ((0, 9),), ((0, 9),), ((3, 6), (0, 3)))
OUT_SCALE = 1.0 / math.sqrt(2.0 * LAYERS)
GELU_C = math.sqrt(2.0 / math.pi)


def iota(shape, dim):
    return lax.broadcasted_iota(I32, shape, dim)


def as_bf16(cond):
    return jnp.where(cond, 1.0, 0.0).astype(BF16)


def dot(a, b):
    return jnp.dot(a, b, preferred_element_type=F32)


def dot_cols(a, b):
    return lax.dot_general(a, b, (((1,), (1,)), ((), ())), preferred_element_type=F32)


def dot_rows(a, b):
    return lax.dot_general(a, b, (((0,), (0,)), ((), ())), preferred_element_type=F32)


def slots_in_lanes(ids):
    t = ids.shape[1]
    e0, e1 = ids[0:1, :], ids[1:2, :]
    experts = iota((NE, t), 0)
    oh0, oh1 = as_bf16(experts == e0), as_bf16(experts == e1)
    earlier = as_bf16(iota((t, t), 0) < iota((t, t), 1))
    c0 = dot(oh0, earlier)
    c1 = dot(oh1, earlier) + jnp.sum(oh0.astype(F32), axis=1, keepdims=True)
    b0 = jnp.sum(c0 * oh0.astype(F32), axis=0, keepdims=True).astype(I32)
    b1 = jnp.sum(c1 * oh1.astype(F32), axis=0, keepdims=True).astype(I32)
    return e0, e1, b0, b1


def in_columns(*rows):
    t = rows[0].shape[1]
    at = iota((t, t), 0)
    stacked = jnp.zeros((t, t), F32)
    for i, row in enumerate(rows):
        stacked = jnp.where(at == i, row, stacked)
    turned = stacked.T
    return [turned[:, i:i + 1] for i in range(len(rows))]


def gelu(v):
    return 0.5 * v * (1.0 + jnp.tanh(GELU_C * (v + 0.044715 * (v * v * v))))


def gelu_slope(v):
    th = jnp.tanh(GELU_C * (v + 0.044715 * (v * v * v)))
    return 0.5 * (1.0 + th) + 0.5 * v * (1.0 - th * th) * (GELU_C * (1.0 + 3.0 * 0.044715 * (v * v)))


def kernel(
    tok_hbm, grad_hbm, idst_ref, codest_ref, wup_hbm, wdown_hbm,
    out_hbm, gtok_hbm, gup_hbm, gdown_hbm,
    tok_ref, grad_ref, out_ref, gtok_ref, gup_ref, gdown_ref,
    send_a, send_b, recv_a, recv_b, back_a, back_b, wup, wdown, xall, gall, hall, pall,
    acc, acc2, fold, wacc,
    a2a_send, a2a_recv, w_send, w_recv, p_send, p_recv, s_send, s_recv, h_send, h_recv, loc, io,
):
    T = tok_ref.shape[0]
    NS = NE * 8
    R = NS + NE
    CW = wup.shape[1]
    dp, me = lax.axis_index("dp"), lax.axis_index("expert")
    x, z = lax.div(me, NZ), lax.rem(me, NZ)
    y, core = lax.div(dp, NCORE), lax.rem(dp, NCORE)
    mate = y * NCORE + (1 - core)

    def peer(k):
        return lax.rem(x + lax.div(k, NZ), NX) * NZ + lax.rem(z + lax.rem(k, NZ), NZ)

    def dpeer(k):
        return lax.rem(dp + k, ND)

    def ypeer(k):
        return lax.rem(y + k, NY) * NCORE + core

    def each(lo, hi, body):
        def step(k, carry):
            body(k)
            return carry
        lax.fori_loop(lo, hi, step, 0)

    def a2a(wave, part, src, dst, k):
        t = peer(k)
        lo, n = PARTS[wave][part]
        sem = (2 * wave + part) * NE + k
        return pltpu.make_async_remote_copy(
            src_ref=src.at[pl.ds(lo, n), pl.ds(pl.multiple_of(t * 8, 8), 8), :],
            dst_ref=dst.at[pl.ds(lo, n), pl.ds(pl.multiple_of(me * 8, 8), 8), :],
            send_sem=a2a_send.at[sem], recv_sem=a2a_recv.at[sem],
            device_id={"expert": t}, device_id_type=MESH)

    def own(wave, part, src, dst):
        lo, n = PARTS[wave][part]
        rows = pl.ds(pl.multiple_of(me * 8, 8), 8)
        return pltpu.make_async_copy(
            src.at[pl.ds(lo, n), rows, :], dst.at[pl.ds(lo, n), rows, :], io.at[8 + 2 * wave + part])

    def start_part(wave, part, src, dst):
        own(wave, part, src, dst).start()
        each(1, NE, lambda k: a2a(wave, part, src, dst, k).start())

    def landed_part(wave, part, src, dst):
        own(wave, part, src, dst).wait()
        each(1, NE, lambda k: a2a(wave, part, src, dst, k).wait_recv())

    def start_wave(wave, src, dst):
        for part in range(len(PARTS[wave])):
            start_part(wave, part, src, dst)

    def landed_wave(wave, src, dst):
        for part in range(len(PARTS[wave])):
            landed_part(wave, part, src, dst)

    def sent_wave(wave, src, dst):
        for part in range(len(PARTS[wave])):
            each(1, NE, lambda k: a2a(wave, part, src, dst, k).wait_send())

    def weight(i, k):
        src, dst = ((wup_hbm, wup), (wdown_hbm, wdown))[i]
        return pltpu.make_async_remote_copy(
            src_ref=src.at[0], dst_ref=dst.at[dp],
            send_sem=w_send.at[i * NY + k], recv_sem=w_recv.at[i * NY + k],
            device_id={"dp": ypeer(k)}, device_id_type=MESH)

    def weight_own(i):
        src, dst = ((wup_hbm, wup), (wdown_hbm, wdown))[i]
        return pltpu.make_async_copy(src.at[0], dst.at[dp], loc.at[4 + i])

    def weight_mate0(i):
        src, dst = ((wup_hbm, wup), (wdown_hbm, wdown))[i]
        return pltpu.make_async_remote_copy(
            src_ref=src.at[0], dst_ref=dst.at[dp],
            send_sem=p_send.at[i * NY], recv_sem=p_recv.at[i * NY],
            device_id={"dp": mate}, device_id_type=MESH)

    def weight_mate(i, k):
        buf = (wup, wdown)[i]
        j = lax.rem(y + NY - k, NY) * NCORE + core
        return pltpu.make_async_remote_copy(
            src_ref=buf.at[j], dst_ref=buf.at[j],
            send_sem=p_send.at[i * NY + k], recv_sem=p_recv.at[i * NY + k],
            device_id={"dp": mate}, device_id_type=MESH)

    def slices(i, k):
        src, dst = ((recv_a, xall), (recv_b, gall))[i]
        t = dpeer(k)
        return pltpu.make_async_remote_copy(
            src_ref=src.at[t], dst_ref=dst.at[dp],
            send_sem=s_send.at[i * ND + k], recv_sem=s_recv.at[i * ND + k],
            device_id={"dp": t}, device_id_type=MESH)

    def slice_own(i):
        src, dst = ((recv_a, xall), (recv_b, gall))[i]
        return pltpu.make_async_copy(src.at[dp], dst.at[dp], loc.at[6 + i])

    def acts(i, k):
        buf = (hall, pall)[i]
        return pltpu.make_async_remote_copy(
            src_ref=buf.at[dp], dst_ref=buf.at[dp],
            send_sem=h_send.at[i * ND + k], recv_sem=h_recv.at[i * ND + k],
            device_id={"dp": dpeer(k)}, device_id_type=MESH)

    tok_in = pltpu.make_async_copy(tok_hbm, tok_ref, io.at[0])
    grad_in = pltpu.make_async_copy(grad_hbm, grad_ref, io.at[1])
    tok_in.start()
    barrier = pltpu.get_barrier_semaphore()
    each(1, NE, lambda k: pl.semaphore_signal(
        barrier, inc=1, device_id={"expert": peer(k)}, device_id_type=MESH))
    each(1, ND, lambda k: pl.semaphore_signal(
        barrier, inc=1, device_id={"dp": dpeer(k)}, device_id_type=MESH))
    grad_in.start()
    weight_own(0).start()
    weight_own(1).start()

    e0, e1, b0, b1 = slots_in_lanes(idst_ref[...])
    s_iota = iota((NS, T), 0)
    s_exp, s_pos = lax.div(s_iota, 8), lax.rem(s_iota, 8)
    m0 = (s_iota == e0 * 8 + b0) & (b0 < 8)
    m1 = (s_iota == e1 * 8 + b1) & (b1 < 8)
    n0 = (s_exp == e0) & (b0 == 8)
    n1 = (s_exp == e1) & (b1 == 8)
    pick = as_bf16(m0 | m1)
    gv0, gv1 = codest_ref[0:1, :].astype(F32), codest_ref[1:2, :].astype(F32)
    gs = gv0 + gv1
    w0, w1 = OUT_SCALE * (gv0 / gs), OUT_SCALE * (gv1 / gs)
    zero = jnp.zeros((), F32)
    scale = jnp.sum(jnp.where(m0, w0, zero) + jnp.where(m1, w1, zero), axis=1, keepdims=True)
    scale9 = jnp.sum(jnp.where(n0, w0, zero) + jnp.where(n1, w1, zero), axis=1, keepdims=True)
    ninth = n0 | n1

    def cols(c):
        return pl.ds(pl.multiple_of(c * CW, 128), CW)

    def gather(src, dst, mul, lo, hi):
        if lo == 0:
            fold[...] = jnp.zeros_like(fold)

        def body(c):
            part = src[:, cols(c)]
            rows = dot(pick, part)
            dst[c] = (rows if mul is None else rows * mul).astype(BF16)
            fold[...] += dot(as_bf16(ninth & (s_pos == c)), part)
        each(lo, hi, body)

    tok_in.wait()
    gather(tok_ref, send_a, None, 0, 4)
    pl.semaphore_wait(barrier, NE - 1 + ND - 1)
    start_part(0, 0, send_a, recv_a)
    gather(tok_ref, send_a, None, 4, ND)
    send_a[ND] = fold[...].astype(BF16)
    start_part(0, 1, send_a, recv_a)
    each(1, NY, lambda k: weight(0, k).start())
    weight_mate0(0).start()
    each(1, NY, lambda k: weight(1, k).start())
    weight_mate0(1).start()
    grad_in.wait()
    gather(grad_ref, send_b, scale, 0, ND)
    send_b[ND] = (fold[...] * scale9).astype(BF16)
    start_wave(1, send_b, recv_b)

    def pass_on(i):
        def body(k):
            weight(i, k).wait_recv()
            weight_mate(i, k).start()
        each(1, NY, body)

    pass_on(0)

    def unfold(buf):
        tail = buf[ND, 0:NS, :]

        def body(c):
            sel = as_bf16(iota((NE, NS), 1) == iota((NE, NS), 0) * 8 + c)
            buf[c, NS:R, :] = dot(sel, tail).astype(BF16)
        each(0, ND, body)

    landed_wave(0, send_a, recv_a)
    unfold(recv_a)
    slice_own(0).start()
    each(1, ND, lambda k: slices(0, k).start())

    weight_own(0).wait()
    weight_mate0(0).wait_recv()
    each(1, NY, lambda k: weight_mate(0, k).wait_recv())

    def contract(dst, rows, mat):
        dst[...] = jnp.zeros_like(dst)

        def body(c):
            dst[...] += dot(rows[c], mat[c])
        each(0, ND, body)

    contract(acc, recv_a, wup)
    hall[dp] = gelu(acc[...]).astype(BF16)
    each(1, ND, lambda k: acts(0, k).start())
    pass_on(1)
    weight_own(1).wait()
    weight_mate0(1).wait_recv()
    each(1, NY, lambda k: weight_mate(1, k).wait_recv())

    def expand(rows, mat, dst):
        fold[...] = jnp.zeros_like(fold)

        def body(c):
            o = dot_cols(rows, mat[c]).astype(BF16)
            dst[c] = o[0:NS]
            put = as_bf16(iota((NS, NE), 0) == iota((NS, NE), 1) * 8 + c)
            fold[...] += dot(put, o[NS:R])
        each(0, ND, body)
        dst[ND] = fold[...].astype(BF16)

    sent_wave(0, send_a, recv_a)
    expand(hall[dp], wdown, send_a)
    start_wave(2, send_a, back_a)

    landed_wave(1, send_b, recv_b)
    unfold(recv_b)
    slice_own(1).start()
    each(1, ND, lambda k: slices(1, k).start())
    contract(acc2, recv_b, wdown)
    pall[dp] = (acc2[...] * gelu_slope(acc[...])).astype(BF16)
    each(1, ND, lambda k: acts(1, k).start())
    sent_wave(1, send_b, recv_b)
    expand(pall[dp], wup, send_b)
    start_wave(3, send_b, back_b)

    def weight_grad(i, act, rows, dst):
        other = (hall, pall)[act]
        slice_own(i).wait()
        each(1, ND, lambda k: slices(i, k).wait_recv())
        each(1, ND, lambda k: acts(act, k).wait_recv())
        wacc[...] = jnp.zeros_like(wacc)

        def body(j):
            wacc[...] += dot_rows(rows[j], other[j])
        each(0, ND, body)
        dst[0] = wacc[...].astype(BF16)

    gdown_out = pltpu.make_async_copy(gdown_ref, gdown_hbm, io.at[2])
    gup_out = pltpu.make_async_copy(gup_ref, gup_hbm, io.at[3])
    weight_grad(1, 0, gall, gdown_ref)
    gdown_out.start()
    weight_grad(0, 1, xall, gup_ref)
    gup_out.start()

    columns = in_columns(e0.astype(F32), e1.astype(F32), b0.astype(F32), b1.astype(F32), w0, w1)
    f0, f1, r0, r1 = [col.astype(I32) for col in columns[:4]]
    v0, v1 = columns[4:]
    t_iota = iota((T, NS), 1)
    q0 = as_bf16((t_iota == f0 * 8 + r0) & (r0 < 8))
    q1 = as_bf16((t_iota == f1 * 8 + r1) & (r1 < 8))
    landed_wave(2, send_a, back_a)

    def mix(c):
        k0 = as_bf16((t_iota == f0 * 8 + c) & (r0 == 8))
        k1 = as_bf16((t_iota == f1 * 8 + c) & (r1 == 8))
        main, tail = back_a[c], back_a[ND]
        first = dot(q0, main) + dot(k0, tail)
        second = dot(q1, main) + dot(k1, tail)
        out_ref[:, cols(c)] = (first * v0 + second * v1).astype(BF16)
    each(0, ND, mix)
    out_out = pltpu.make_async_copy(out_ref, out_hbm, io.at[4])
    out_out.start()

    qs = q0 + q1

    def mix_grad(c):
        ks = as_bf16(((t_iota == f0 * 8 + c) & (r0 == 8)) | ((t_iota == f1 * 8 + c) & (r1 == 8)))
        gtok_ref[:, cols(c)] = (dot(qs, back_b[c]) + dot(ks, back_b[ND])).astype(BF16)

    def gtok_out(part, lo, hi):
        at = pl.ds(lo * CW, (hi - lo) * CW)
        return pltpu.make_async_copy(gtok_ref.at[:, at], gtok_hbm.at[:, at], io.at[5 + part])

    landed_part(3, 0, send_b, back_b)
    each(3, ND, mix_grad)
    gtok_out(0, 3, ND).start()
    landed_part(3, 1, send_b, back_b)
    each(0, 3, mix_grad)
    gtok_out(1, 0, 3).start()

    sent_wave(2, send_a, back_a)
    sent_wave(3, send_b, back_b)
    for i in (0, 1):
        each(1, NY, lambda k: weight(i, k).wait_send())
        weight_mate0(i).wait_send()
        each(1, NY, lambda k: weight_mate(i, k).wait_send())
        each(1, ND, lambda k: slices(i, k).wait_send())
        each(1, ND, lambda k: acts(i, k).wait_send())
    gdown_out.wait()
    gup_out.wait()
    out_out.wait()
    gtok_out(0, 3, ND).wait()
    gtok_out(1, 0, 3).wait()


def hand_on_kernel(*refs):
    n = len(refs) // 3
    src, dst, held, sem = refs[:n], refs[n:2 * n], refs[2 * n:3 * n], refs[3 * n]
    into = [pltpu.make_async_copy(src[i], held[i], sem.at[i]) for i in range(n)]
    out = [pltpu.make_async_copy(held[i], dst[i], sem.at[n + i]) for i in range(n)]
    for c in into:
        c.start()
    for i in range(n):
        into[i].wait()
        out[i].start()
    for c in out:
        c.wait()


def hand_on(*arrays):
    n = len(arrays)
    hbm = pl.BlockSpec(memory_space=pl.ANY)
    return pl.pallas_call(
        hand_on_kernel,
        name="hand_on",
        out_shape=tuple(jax.ShapeDtypeStruct(a.shape, a.dtype) for a in arrays),
        in_specs=[hbm] * n,
        out_specs=(hbm,) * n,
        scratch_shapes=[pltpu.VMEM(a.shape, a.dtype) for a in arrays] + [pltpu.SemaphoreType.DMA((2 * n,))],
        compiler_params=pltpu.CompilerParams(vmem_limit_bytes=67043328),
    )(*arrays)


def local(tokens, grad_out, expert_ids, gate_codes, w_up, w_down):
    t, d = tokens.shape
    cw, h = w_up.shape[1], w_up.shape[2]
    ns, r = NE * 8, NE * 9
    vmem = pl.BlockSpec(memory_space=pltpu.VMEM)
    hbm = pl.BlockSpec(memory_space=pl.ANY)
    dma = pltpu.SemaphoreType.DMA
    outs = pl.pallas_call(
        kernel,
        name="moe",
        out_shape=(
            jax.ShapeDtypeStruct((t, d), BF16),
            jax.ShapeDtypeStruct((t, d), BF16),
            jax.ShapeDtypeStruct((1, cw, h), BF16),
            jax.ShapeDtypeStruct((1, cw, h), BF16),
        ),
        in_specs=[hbm] * 2 + [vmem] * 2 + [hbm] * 2,
        out_specs=(hbm,) * 4,
        scratch_shapes=[
            pltpu.VMEM((t, d), BF16), pltpu.VMEM((t, d), BF16),
            pltpu.VMEM((t, d), BF16), pltpu.VMEM((t, d), BF16),
            pltpu.VMEM((1, cw, h), BF16), pltpu.VMEM((1, cw, h), BF16),
            pltpu.VMEM((ND + 1, ns, cw), BF16), pltpu.VMEM((ND + 1, ns, cw), BF16),
            pltpu.VMEM((ND + 1, r, cw), BF16), pltpu.VMEM((ND + 1, r, cw), BF16),
            pltpu.VMEM((ND + 1, ns, cw), BF16), pltpu.VMEM((ND + 1, ns, cw), BF16),
            pltpu.VMEM((ND, cw, h), BF16), pltpu.VMEM((ND, cw, h), BF16),
            pltpu.VMEM((ND, r, cw), BF16), pltpu.VMEM((ND, r, cw), BF16),
            pltpu.VMEM((ND, r, h), BF16), pltpu.VMEM((ND, r, h), BF16),
            pltpu.VMEM((r, h), F32), pltpu.VMEM((r, h), F32),
            pltpu.VMEM((ns, cw), F32), pltpu.VMEM((cw, h), F32),
            dma((8 * NE,)), dma((8 * NE,)), dma((2 * NY,)), dma((2 * NY,)),
            dma((2 * NY,)), dma((2 * NY,)), dma((2 * ND,)), dma((2 * ND,)),
            dma((2 * ND,)), dma((2 * ND,)), dma((8,)), dma((16,)),
        ],
        compiler_params=pltpu.CompilerParams(
            collective_id=0, has_side_effects=True, vmem_limit_bytes=67043328),
    )(tokens, grad_out, expert_ids.T, gate_codes.T, w_up, w_down)
    return hand_on(*outs)


def solution(mesh):
    rows = P(("dp", "expert"), None)
    shard = P("expert", "dp", None)
    return jax.shard_map(
        local, mesh=mesh, in_specs=(rows,) * 4 + (shard,) * 2,
        out_specs=(rows, rows, shard, shard), check_vma=False)
```

```python
import functools
import math

import jax
import jax.numpy as jnp
from jax import lax
from jax.experimental import pallas as pl
from jax.experimental.pallas import tpu as pltpu
from jax.sharding import PartitionSpec as P

LAYERS = 40
NX, NZ = 4, 8
NY, NCORE = 4, 2
NE, ND = NX * NZ, NY * NCORE
MESH = pl.DeviceIdType.MESH
F32, BF16, I32 = jnp.float32, jnp.bfloat16, jnp.int32
PARTS = (((0, 2), (2, 7)), ((0, 9),), ((0, 9),), ((1, 8), (0, 1)))
PIECES = 4
OUT_SCALE = 1.0 / math.sqrt(2.0 * LAYERS)
GELU_C = math.sqrt(2.0 / math.pi)


def iota(shape, dim):
    return lax.broadcasted_iota(I32, shape, dim)


def as_bf16(cond):
    return jnp.where(cond, 1.0, 0.0).astype(BF16)


def dot(a, b):
    return jnp.dot(a, b, preferred_element_type=F32)


def dot_cols(a, b):
    return lax.dot_general(a, b, (((1,), (1,)), ((), ())), preferred_element_type=F32)


def dot_rows(a, b):
    return lax.dot_general(a, b, (((0,), (0,)), ((), ())), preferred_element_type=F32)


def slots_in_lanes(ids):
    t = ids.shape[1]
    e0, e1 = ids[0:1, :], ids[1:2, :]
    experts = iota((NE, t), 0)
    oh0, oh1 = as_bf16(experts == e0), as_bf16(experts == e1)
    earlier = as_bf16(iota((t, t), 0) < iota((t, t), 1))
    c0 = dot(oh0, earlier)
    c1 = dot(oh1, earlier) + jnp.sum(oh0.astype(F32), axis=1, keepdims=True)
    b0 = jnp.sum(c0 * oh0.astype(F32), axis=0, keepdims=True).astype(I32)
    b1 = jnp.sum(c1 * oh1.astype(F32), axis=0, keepdims=True).astype(I32)
    return e0, e1, b0, b1


def in_columns(*rows):
    t = rows[0].shape[1]
    at = iota((t, t), 0)
    stacked = jnp.zeros((t, t), F32)
    for i, row in enumerate(rows):
        stacked = jnp.where(at == i, row, stacked)
    turned = stacked.T
    return [turned[:, i:i + 1] for i in range(len(rows))]


def gelu(v):
    return 0.5 * v * (1.0 + jnp.tanh(GELU_C * (v + 0.044715 * (v * v * v))))


def gelu_slope(v):
    th = jnp.tanh(GELU_C * (v + 0.044715 * (v * v * v)))
    return 0.5 * (1.0 + th) + 0.5 * v * (1.0 - th * th) * (GELU_C * (1.0 + 3.0 * 0.044715 * (v * v)))


def kernel(
    tok_hbm, grad_hbm, idst_ref, codest_ref, wup_hbm, wdown_hbm,
    out_hbm, gtok_hbm, gup_hbm, gdown_hbm,
    tok_ref, grad_ref, out_ref, gtok_ref, gup_ref, gdown_ref,
    send_a, send_b, recv_a, recv_b, back_a, back_b, wup, wdown, xall, gall, hall, pall,
    acc, acc2, fold, wacc,
    a2a_send, a2a_recv, w_send, w_recv, p_send, p_recv, s_send, s_recv, h_send, h_recv, loc, io,
):
    T = tok_ref.shape[0]
    NS = NE * 8
    R = NS + NE
    CW = wup.shape[1]
    dp, me = lax.axis_index("dp"), lax.axis_index("expert")
    x, z = lax.div(me, NZ), lax.rem(me, NZ)
    y, core = lax.div(dp, NCORE), lax.rem(dp, NCORE)
    mate = y * NCORE + (1 - core)

    def peer(k):
        i, j = lax.div(k, NZ), lax.rem(k, NZ)
        odd = lax.rem(j, 2)
        dz = odd * (NZ // 2 + lax.div(j + 1, 2)) + (1 - odd) * (NZ // 2 - lax.div(j, 2))
        return lax.rem(x + (NX - 1) - i, NX) * NZ + lax.rem(z + dz, NZ)

    def dpeer(k):
        return lax.rem(dp + k, ND)

    def ypeer(k):
        return lax.rem(y + k, NY) * NCORE + core

    def each(lo, hi, body):
        def step(k, carry):
            body(k)
            return carry
        lax.fori_loop(lo, hi, step, 0)

    def a2a(wave, part, src, dst, k):
        t = peer(k)
        lo, n = PARTS[wave][part]
        sem = (2 * wave + part) * NE + k
        return pltpu.make_async_remote_copy(
            src_ref=src.at[pl.ds(lo, n), pl.ds(pl.multiple_of(t * 8, 8), 8), :],
            dst_ref=dst.at[pl.ds(lo, n), pl.ds(pl.multiple_of(me * 8, 8), 8), :],
            send_sem=a2a_send.at[sem], recv_sem=a2a_recv.at[sem],
            device_id={"expert": t}, device_id_type=MESH)

    def own(wave, part, src, dst):
        lo, n = PARTS[wave][part]
        rows = pl.ds(pl.multiple_of(me * 8, 8), 8)
        return pltpu.make_async_copy(
            src.at[pl.ds(lo, n), rows, :], dst.at[pl.ds(lo, n), rows, :], io.at[8 + 2 * wave + part])

    def start_part(wave, part, src, dst):
        own(wave, part, src, dst).start()
        each(0, NE - 1, lambda k: a2a(wave, part, src, dst, k).start())

    def landed_part(wave, part, src, dst):
        own(wave, part, src, dst).wait()
        each(0, NE - 1, lambda k: a2a(wave, part, src, dst, k).wait_recv())

    def start_wave(wave, src, dst):
        for part in range(len(PARTS[wave])):
            start_part(wave, part, src, dst)

    def landed_wave(wave, src, dst):
        for part in range(len(PARTS[wave])):
            landed_part(wave, part, src, dst)

    def sent_wave(wave, src, dst):
        for part in range(len(PARTS[wave])):
            each(0, NE - 1, lambda k: a2a(wave, part, src, dst, k).wait_send())

    def weight(i, k):
        src, dst = ((wup_hbm, wup), (wdown_hbm, wdown))[i]
        return pltpu.make_async_remote_copy(
            src_ref=src.at[0], dst_ref=dst.at[dp],
            send_sem=w_send.at[i * NY + k], recv_sem=w_recv.at[i * NY + k],
            device_id={"dp": ypeer(k)}, device_id_type=MESH)

    def weight_own(i):
        src, dst = ((wup_hbm, wup), (wdown_hbm, wdown))[i]
        return pltpu.make_async_copy(src.at[0], dst.at[dp], loc.at[4 + i])

    def weight_mate0(i):
        src, dst = ((wup_hbm, wup), (wdown_hbm, wdown))[i]
        return pltpu.make_async_remote_copy(
            src_ref=src.at[0], dst_ref=dst.at[dp],
            send_sem=p_send.at[i * NY], recv_sem=p_recv.at[i * NY],
            device_id={"dp": mate}, device_id_type=MESH)

    def weight_mate(i, k):
        buf = (wup, wdown)[i]
        j = lax.rem(y + NY - k, NY) * NCORE + core
        return pltpu.make_async_remote_copy(
            src_ref=buf.at[j], dst_ref=buf.at[j],
            send_sem=p_send.at[i * NY + k], recv_sem=p_recv.at[i * NY + k],
            device_id={"dp": mate}, device_id_type=MESH)

    def slices(i, k):
        src, dst = ((recv_a, xall), (recv_b, gall))[i]
        t = dpeer(k)
        return pltpu.make_async_remote_copy(
            src_ref=src.at[t], dst_ref=dst.at[dp],
            send_sem=s_send.at[i * ND + k], recv_sem=s_recv.at[i * ND + k],
            device_id={"dp": t}, device_id_type=MESH)

    def slice_own(i):
        src, dst = ((recv_a, xall), (recv_b, gall))[i]
        return pltpu.make_async_copy(src.at[dp], dst.at[dp], loc.at[6 + i])

    def acts(i, k):
        buf = (hall, pall)[i]
        return pltpu.make_async_remote_copy(
            src_ref=buf.at[dp], dst_ref=buf.at[dp],
            send_sem=h_send.at[i * ND + k], recv_sem=h_recv.at[i * ND + k],
            device_id={"dp": dpeer(k)}, device_id_type=MESH)

    tok_in = pltpu.make_async_copy(tok_hbm, tok_ref, io.at[0])
    grad_in = pltpu.make_async_copy(grad_hbm, grad_ref, io.at[1])
    tok_in.start()
    barrier = pltpu.get_barrier_semaphore()
    each(0, NE - 1, lambda k: pl.semaphore_signal(
        barrier, inc=1, device_id={"expert": peer(k)}, device_id_type=MESH))
    each(1, ND, lambda k: pl.semaphore_signal(
        barrier, inc=1, device_id={"dp": dpeer(k)}, device_id_type=MESH))
    grad_in.start()
    weight_own(0).start()
    weight_own(1).start()

    e0, e1, b0, b1 = slots_in_lanes(idst_ref[...])
    s_iota = iota((NS, T), 0)
    s_exp, s_pos = lax.div(s_iota, 8), lax.rem(s_iota, 8)
    m0 = (s_iota == e0 * 8 + b0) & (b0 < 8)
    m1 = (s_iota == e1 * 8 + b1) & (b1 < 8)
    n0 = (s_exp == e0) & (b0 == 8)
    n1 = (s_exp == e1) & (b1 == 8)
    pick = as_bf16(m0 | m1)
    gv0, gv1 = codest_ref[0:1, :].astype(F32), codest_ref[1:2, :].astype(F32)
    gs = gv0 + gv1
    w0, w1 = OUT_SCALE * (gv0 / gs), OUT_SCALE * (gv1 / gs)
    zero = jnp.zeros((), F32)
    scale = jnp.sum(jnp.where(m0, w0, zero) + jnp.where(m1, w1, zero), axis=1, keepdims=True)
    scale9 = jnp.sum(jnp.where(n0, w0, zero) + jnp.where(n1, w1, zero), axis=1, keepdims=True)
    ninth = n0 | n1

    def cols(c):
        return pl.ds(pl.multiple_of(c * CW, 128), CW)

    def gather(src, dst, mul, lo, hi):
        if lo == 0:
            fold[...] = jnp.zeros_like(fold)

        def body(c):
            part = src[:, cols(c)]
            rows = dot(pick, part)
            dst[c] = (rows if mul is None else rows * mul).astype(BF16)
            fold[...] += dot(as_bf16(ninth & (s_pos == c)), part)
        each(lo, hi, body)

    tok_in.wait()
    gather(tok_ref, send_a, None, 0, 2)
    pl.semaphore_wait(barrier, NE - 1 + ND - 1)
    start_part(0, 0, send_a, recv_a)
    gather(tok_ref, send_a, None, 2, ND)
    send_a[ND] = fold[...].astype(BF16)
    start_part(0, 1, send_a, recv_a)
    each(1, NY, lambda k: weight(0, k).start())
    weight_mate0(0).start()
    each(1, NY, lambda k: weight(1, k).start())
    weight_mate0(1).start()
    grad_in.wait()
    gather(grad_ref, send_b, scale, 0, ND)
    send_b[ND] = (fold[...] * scale9).astype(BF16)
    start_wave(1, send_b, recv_b)

    def pass_on(i):
        def body(k):
            weight(i, k).wait_recv()
            weight_mate(i, k).start()
        each(1, NY, body)

    pass_on(0)

    def unfold(buf):
        tail = buf[ND, 0:NS, :]

        def body(c):
            sel = as_bf16(iota((NE, NS), 1) == iota((NE, NS), 0) * 8 + c)
            buf[c, NS:R, :] = dot(sel, tail).astype(BF16)
        each(0, ND, body)

    landed_wave(0, send_a, recv_a)
    unfold(recv_a)
    slice_own(0).start()
    each(1, ND, lambda k: slices(0, k).start())

    weight_own(0).wait()
    weight_mate0(0).wait_recv()
    each(1, NY, lambda k: weight_mate(0, k).wait_recv())

    def contract(dst, rows, mat):
        dst[...] = jnp.zeros_like(dst)

        def body(c):
            dst[...] += dot(rows[c], mat[c])
        each(0, ND, body)

    contract(acc, recv_a, wup)
    hall[dp] = gelu(acc[...]).astype(BF16)
    each(1, ND, lambda k: acts(0, k).start())
    pass_on(1)
    weight_own(1).wait()
    weight_mate0(1).wait_recv()
    each(1, NY, lambda k: weight_mate(1, k).wait_recv())

    def expand(rows, mat, dst):
        fold[...] = jnp.zeros_like(fold)

        def body(c):
            o = dot_cols(rows, mat[c]).astype(BF16)
            dst[c] = o[0:NS]
            put = as_bf16(iota((NS, NE), 0) == iota((NS, NE), 1) * 8 + c)
            fold[...] += dot(put, o[NS:R])
        each(0, ND, body)
        dst[ND] = fold[...].astype(BF16)

    sent_wave(0, send_a, recv_a)
    expand(hall[dp], wdown, send_a)
    start_wave(2, send_a, back_a)

    landed_wave(1, send_b, recv_b)
    unfold(recv_b)
    slice_own(1).start()
    each(1, ND, lambda k: slices(1, k).start())
    contract(acc2, recv_b, wdown)
    pall[dp] = (acc2[...] * gelu_slope(acc[...])).astype(BF16)
    each(1, ND, lambda k: acts(1, k).start())
    sent_wave(1, send_b, recv_b)
    expand(pall[dp], wup, send_b)
    start_wave(3, send_b, back_b)

    def weight_grad(i, act, rows, dst):
        other = (hall, pall)[act]
        slice_own(i).wait()
        each(1, ND, lambda k: slices(i, k).wait_recv())
        each(1, ND, lambda k: acts(act, k).wait_recv())
        wacc[...] = jnp.zeros_like(wacc)

        def body(j):
            wacc[...] += dot_rows(rows[j], other[j])
        each(0, ND, body)
        dst[0] = wacc[...].astype(BF16)

    gdown_out = pltpu.make_async_copy(gdown_ref, gdown_hbm, io.at[2])
    gup_out = pltpu.make_async_copy(gup_ref, gup_hbm, io.at[3])
    weight_grad(1, 0, gall, gdown_ref)
    gdown_out.start()
    weight_grad(0, 1, xall, gup_ref)
    gup_out.start()

    columns = in_columns(e0.astype(F32), e1.astype(F32), b0.astype(F32), b1.astype(F32), w0, w1)
    f0, f1, r0, r1 = [col.astype(I32) for col in columns[:4]]
    v0, v1 = columns[4:]
    t_iota = iota((T, NS), 1)
    q0 = as_bf16((t_iota == f0 * 8 + r0) & (r0 < 8))
    q1 = as_bf16((t_iota == f1 * 8 + r1) & (r1 < 8))
    landed_wave(2, send_a, back_a)

    def mix(c):
        k0 = as_bf16((t_iota == f0 * 8 + c) & (r0 == 8))
        k1 = as_bf16((t_iota == f1 * 8 + c) & (r1 == 8))
        main, tail = back_a[c], back_a[ND]
        first = dot(q0, main) + dot(k0, tail)
        second = dot(q1, main) + dot(k1, tail)
        out_ref[:, cols(c)] = (first * v0 + second * v1).astype(BF16)
    each(0, ND, mix)
    out_out = pltpu.make_async_copy(out_ref, out_hbm, io.at[4])
    out_out.start()

    qs = q0 + q1

    def mix_grad(c):
        ks = as_bf16(((t_iota == f0 * 8 + c) & (r0 == 8)) | ((t_iota == f1 * 8 + c) & (r1 == 8)))
        gtok_ref[:, cols(c)] = (dot(qs, back_b[c]) + dot(ks, back_b[ND])).astype(BF16)

    def gtok_out(part, lo, hi):
        at = pl.ds(lo * CW, (hi - lo) * CW)
        return pltpu.make_async_copy(gtok_ref.at[:, at], gtok_hbm.at[:, at], io.at[5 + part])

    landed_part(3, 0, send_b, back_b)
    each(1, ND, mix_grad)
    gtok_out(0, 1, ND).start()
    landed_part(3, 1, send_b, back_b)
    each(0, 1, mix_grad)
    gtok_out(1, 0, 1).start()

    sent_wave(2, send_a, back_a)
    sent_wave(3, send_b, back_b)
    for i in (0, 1):
        each(1, NY, lambda k: weight(i, k).wait_send())
        weight_mate0(i).wait_send()
        each(1, NY, lambda k: weight_mate(i, k).wait_send())
        each(1, ND, lambda k: slices(i, k).wait_send())
        each(1, ND, lambda k: acts(i, k).wait_send())
    gdown_out.wait()
    gup_out.wait()
    out_out.wait()
    gtok_out(0, 1, ND).wait()
    gtok_out(1, 0, 1).wait()


def hand_on_kernel(*refs):
    n = len(refs) // 3
    src, dst, held, sem = refs[:n], refs[n:2 * n], refs[2 * n:3 * n], refs[3 * n]
    into, out = [], []
    for i in range(n):
        rows = src[i].shape[0] // PIECES
        for j in range(PIECES):
            at, s = pl.ds(j * rows, rows), 2 * (i * PIECES + j)
            into.append(pltpu.make_async_copy(src[i].at[at], held[i].at[at], sem.at[s]))
            out.append(pltpu.make_async_copy(held[i].at[at], dst[i].at[at], sem.at[s + 1]))
    for c in into:
        c.start()
    for c, d in zip(into, out):
        c.wait()
        d.start()
    for d in out:
        d.wait()


def hand_on(*arrays):
    n = len(arrays)
    hbm = pl.BlockSpec(memory_space=pl.ANY)
    return pl.pallas_call(
        hand_on_kernel,
        name="hand_on",
        out_shape=tuple(jax.ShapeDtypeStruct(a.shape, a.dtype) for a in arrays),
        in_specs=[hbm] * n,
        out_specs=(hbm,) * n,
        scratch_shapes=[pltpu.VMEM(a.shape, a.dtype) for a in arrays] + [pltpu.SemaphoreType.DMA((2 * n * PIECES,))],
        compiler_params=pltpu.CompilerParams(vmem_limit_bytes=67043328),
    )(*arrays)


def local(tokens, grad_out, expert_ids, gate_codes, w_up, w_down):
    t, d = tokens.shape
    cw, h = w_up.shape[1], w_up.shape[2]
    ns, r = NE * 8, NE * 9
    vmem = pl.BlockSpec(memory_space=pltpu.VMEM)
    hbm = pl.BlockSpec(memory_space=pl.ANY)
    dma = pltpu.SemaphoreType.DMA
    outs = pl.pallas_call(
        kernel,
        name="moe",
        out_shape=(
            jax.ShapeDtypeStruct((t, d), BF16),
            jax.ShapeDtypeStruct((t, d), BF16),
            jax.ShapeDtypeStruct((1, cw, h), BF16),
            jax.ShapeDtypeStruct((1, cw, h), BF16),
        ),
        in_specs=[hbm] * 2 + [vmem] * 2 + [hbm] * 2,
        out_specs=(hbm,) * 4,
        scratch_shapes=[
            pltpu.VMEM((t, d), BF16), pltpu.VMEM((t, d), BF16),
            pltpu.VMEM((t, d), BF16), pltpu.VMEM((t, d), BF16),
            pltpu.VMEM((1, cw, h), BF16), pltpu.VMEM((1, cw, h), BF16),
            pltpu.VMEM((ND + 1, ns, cw), BF16), pltpu.VMEM((ND + 1, ns, cw), BF16),
            pltpu.VMEM((ND + 1, r, cw), BF16), pltpu.VMEM((ND + 1, r, cw), BF16),
            pltpu.VMEM((ND + 1, ns, cw), BF16), pltpu.VMEM((ND + 1, ns, cw), BF16),
            pltpu.VMEM((ND, cw, h), BF16), pltpu.VMEM((ND, cw, h), BF16),
            pltpu.VMEM((ND, r, cw), BF16), pltpu.VMEM((ND, r, cw), BF16),
            pltpu.VMEM((ND, r, h), BF16), pltpu.VMEM((ND, r, h), BF16),
            pltpu.VMEM((r, h), F32), pltpu.VMEM((r, h), F32),
            pltpu.VMEM((ns, cw), F32), pltpu.VMEM((cw, h), F32),
            dma((8 * NE,)), dma((8 * NE,)), dma((2 * NY,)), dma((2 * NY,)),
            dma((2 * NY,)), dma((2 * NY,)), dma((2 * ND,)), dma((2 * ND,)),
            dma((2 * ND,)), dma((2 * ND,)), dma((8,)), dma((16,)),
        ],
        compiler_params=pltpu.CompilerParams(
            collective_id=0, has_side_effects=True, vmem_limit_bytes=67043328),
    )(tokens, grad_out, expert_ids.T, gate_codes.T, w_up, w_down)
    out, gtok, gup, gdown = outs
    out, gtok, gup, gdown = hand_on(out, gtok, gup[0], gdown[0])
    return out, gtok, gup[None], gdown[None]


def solution(mesh):
    rows = P(("dp", "expert"), None)
    shard = P("expert", "dp", None)
    return jax.shard_map(
        local, mesh=mesh, in_specs=(rows,) * 4 + (shard,) * 2,
        out_specs=(rows, rows, shard, shard), check_vma=False)
```

```python
import functools
import math

import jax
import jax.numpy as jnp
from jax import lax
from jax.experimental import pallas as pl
from jax.experimental.pallas import tpu as pltpu
from jax.sharding import PartitionSpec as P

LAYERS = 40
NX, NZ = 4, 8
NY, NCORE = 4, 2
NE, ND = NX * NZ, NY * NCORE
MESH = pl.DeviceIdType.MESH
F32, BF16, I32 = jnp.float32, jnp.bfloat16, jnp.int32
PARTS = (((0, 4), (4, 5)), ((0, 9),), ((0, 9),), ((3, 6), (0, 3)))
OUT_SCALE = 1.0 / math.sqrt(2.0 * LAYERS)
GELU_C = math.sqrt(2.0 / math.pi)


def iota(shape, dim):
    return lax.broadcasted_iota(I32, shape, dim)


def as_bf16(cond):
    return jnp.where(cond, 1.0, 0.0).astype(BF16)


def dot(a, b):
    return jnp.dot(a, b, preferred_element_type=F32)


def dot_cols(a, b):
    return lax.dot_general(a, b, (((1,), (1,)), ((), ())), preferred_element_type=F32)


def dot_rows(a, b):
    return lax.dot_general(a, b, (((0,), (0,)), ((), ())), preferred_element_type=F32)


def slots_in_lanes(ids):
    t = ids.shape[1]
    e0, e1 = ids[0:1, :], ids[1:2, :]
    experts = iota((NE, t), 0)
    oh0, oh1 = as_bf16(experts == e0), as_bf16(experts == e1)
    earlier = as_bf16(iota((t, t), 0) < iota((t, t), 1))
    c0 = dot(oh0, earlier)
    c1 = dot(oh1, earlier) + jnp.sum(oh0.astype(F32), axis=1, keepdims=True)
    b0 = jnp.sum(c0 * oh0.astype(F32), axis=0, keepdims=True).astype(I32)
    b1 = jnp.sum(c1 * oh1.astype(F32), axis=0, keepdims=True).astype(I32)
    return e0, e1, b0, b1


def in_columns(*rows):
    t = rows[0].shape[1]
    at = iota((t, t), 0)
    stacked = jnp.zeros((t, t), F32)
    for i, row in enumerate(rows):
        stacked = jnp.where(at == i, row, stacked)
    turned = stacked.T
    return [turned[:, i:i + 1] for i in range(len(rows))]


def gelu(v):
    return 0.5 * v * (1.0 + jnp.tanh(GELU_C * (v + 0.044715 * (v * v * v))))


def gelu_slope(v):
    th = jnp.tanh(GELU_C * (v + 0.044715 * (v * v * v)))
    return 0.5 * (1.0 + th) + 0.5 * v * (1.0 - th * th) * (GELU_C * (1.0 + 3.0 * 0.044715 * (v * v)))


def kernel(
    tok_hbm, grad_hbm, idst_ref, codest_ref, wup_hbm, wdown_hbm,
    out_ref, gtok_ref, gup_ref, gdown_ref,
    tok_ref, grad_ref,
    send_a, send_b, recv_a, recv_b, back_a, back_b, wup, wdown, xall, gall, hall, pall,
    acc, acc2, fold, wacc,
    a2a_send, a2a_recv, w_send, w_recv, p_send, p_recv, s_send, s_recv, h_send, h_recv, loc, io,
):
    T = tok_ref.shape[0]
    NS = NE * 8
    R = NS + NE
    CW = wup.shape[1]
    dp, me = lax.axis_index("dp"), lax.axis_index("expert")
    x, z = lax.div(me, NZ), lax.rem(me, NZ)
    y, core = lax.div(dp, NCORE), lax.rem(dp, NCORE)
    mate = y * NCORE + (1 - core)

    def peer(k):
        return lax.rem(x + lax.div(k, NZ), NX) * NZ + lax.rem(z + lax.rem(k, NZ), NZ)

    def dpeer(k):
        return lax.rem(dp + k, ND)

    def ypeer(k):
        return lax.rem(y + k, NY) * NCORE + core

    def each(lo, hi, body):
        def step(k, carry):
            body(k)
            return carry
        lax.fori_loop(lo, hi, step, 0)

    def a2a(wave, part, src, dst, k):
        t = peer(k)
        lo, n = PARTS[wave][part]
        sem = (2 * wave + part) * NE + k
        return pltpu.make_async_remote_copy(
            src_ref=src.at[pl.ds(lo, n), pl.ds(pl.multiple_of(t * 8, 8), 8), :],
            dst_ref=dst.at[pl.ds(lo, n), pl.ds(pl.multiple_of(me * 8, 8), 8), :],
            send_sem=a2a_send.at[sem], recv_sem=a2a_recv.at[sem],
            device_id={"expert": t}, device_id_type=MESH)

    def own(wave, part, src, dst):
        lo, n = PARTS[wave][part]
        rows = pl.ds(pl.multiple_of(me * 8, 8), 8)
        return pltpu.make_async_copy(
            src.at[pl.ds(lo, n), rows, :], dst.at[pl.ds(lo, n), rows, :], io.at[8 + 2 * wave + part])

    def start_part(wave, part, src, dst):
        own(wave, part, src, dst).start()
        each(1, NE, lambda k: a2a(wave, part, src, dst, k).start())

    def landed_part(wave, part, src, dst):
        own(wave, part, src, dst).wait()
        each(1, NE, lambda k: a2a(wave, part, src, dst, k).wait_recv())

    def start_wave(wave, src, dst):
        for part in range(len(PARTS[wave])):
            start_part(wave, part, src, dst)

    def landed_wave(wave, src, dst):
        for part in range(len(PARTS[wave])):
            landed_part(wave, part, src, dst)

    def sent_wave(wave, src, dst):
        for part in range(len(PARTS[wave])):
            each(1, NE, lambda k: a2a(wave, part, src, dst, k).wait_send())

    def weight(i, k):
        src, dst = ((wup_hbm, wup), (wdown_hbm, wdown))[i]
        return pltpu.make_async_remote_copy(
            src_ref=src.at[0], dst_ref=dst.at[dp],
            send_sem=w_send.at[i * NY + k], recv_sem=w_recv.at[i * NY + k],
            device_id={"dp": ypeer(k)}, device_id_type=MESH)

    def weight_own(i):
        src, dst = ((wup_hbm, wup), (wdown_hbm, wdown))[i]
        return pltpu.make_async_copy(src.at[0], dst.at[dp], loc.at[4 + i])

    def weight_mate0(i):
        src, dst = ((wup_hbm, wup), (wdown_hbm, wdown))[i]
        return pltpu.make_async_remote_copy(
            src_ref=src.at[0], dst_ref=dst.at[dp],
            send_sem=p_send.at[i * NY], recv_sem=p_recv.at[i * NY],
            device_id={"dp": mate}, device_id_type=MESH)

    def weight_mate(i, k):
        buf = (wup, wdown)[i]
        j = lax.rem(y + NY - k, NY) * NCORE + core
        return pltpu.make_async_remote_copy(
            src_ref=buf.at[j], dst_ref=buf.at[j],
            send_sem=p_send.at[i * NY + k], recv_sem=p_recv.at[i * NY + k],
            device_id={"dp": mate}, device_id_type=MESH)

    def slices(i, k):
        src, dst = ((recv_a, xall), (recv_b, gall))[i]
        t = dpeer(k)
        return pltpu.make_async_remote_copy(
            src_ref=src.at[t], dst_ref=dst.at[dp],
            send_sem=s_send.at[i * ND + k], recv_sem=s_recv.at[i * ND + k],
            device_id={"dp": t}, device_id_type=MESH)

    def slice_own(i):
        src, dst = ((recv_a, xall), (recv_b, gall))[i]
        return pltpu.make_async_copy(src.at[dp], dst.at[dp], loc.at[6 + i])

    def acts(i, k):
        buf = (hall, pall)[i]
        return pltpu.make_async_remote_copy(
            src_ref=buf.at[dp], dst_ref=buf.at[dp],
            send_sem=h_send.at[i * ND + k], recv_sem=h_recv.at[i * ND + k],
            device_id={"dp": dpeer(k)}, device_id_type=MESH)

    tok_in = pltpu.make_async_copy(tok_hbm, tok_ref, io.at[0])
    grad_in = pltpu.make_async_copy(grad_hbm, grad_ref, io.at[1])
    tok_in.start()
    barrier = pltpu.get_barrier_semaphore()
    each(1, NE, lambda k: pl.semaphore_signal(
        barrier, inc=1, device_id={"expert": peer(k)}, device_id_type=MESH))
    each(1, ND, lambda k: pl.semaphore_signal(
        barrier, inc=1, device_id={"dp": dpeer(k)}, device_id_type=MESH))
    grad_in.start()
    weight_own(0).start()
    weight_own(1).start()

    e0, e1, b0, b1 = slots_in_lanes(idst_ref[...])
    s_iota = iota((NS, T), 0)
    s_exp, s_pos = lax.div(s_iota, 8), lax.rem(s_iota, 8)
    m0 = (s_iota == e0 * 8 + b0) & (b0 < 8)
    m1 = (s_iota == e1 * 8 + b1) & (b1 < 8)
    n0 = (s_exp == e0) & (b0 == 8)
    n1 = (s_exp == e1) & (b1 == 8)
    pick = as_bf16(m0 | m1)
    gv0, gv1 = codest_ref[0:1, :].astype(F32), codest_ref[1:2, :].astype(F32)
    gs = gv0 + gv1
    w0, w1 = OUT_SCALE * (gv0 / gs), OUT_SCALE * (gv1 / gs)
    zero = jnp.zeros((), F32)
    scale = jnp.sum(jnp.where(m0, w0, zero) + jnp.where(m1, w1, zero), axis=1, keepdims=True)
    scale9 = jnp.sum(jnp.where(n0, w0, zero) + jnp.where(n1, w1, zero), axis=1, keepdims=True)
    ninth = n0 | n1

    def cols(c):
        return pl.ds(pl.multiple_of(c * CW, 128), CW)

    def gather(src, dst, mul, lo, hi):
        if lo == 0:
            fold[...] = jnp.zeros_like(fold)

        def body(c):
            part = src[:, cols(c)]
            rows = dot(pick, part)
            dst[c] = (rows if mul is None else rows * mul).astype(BF16)
            fold[...] += dot(as_bf16(ninth & (s_pos == c)), part)
        each(lo, hi, body)

    tok_in.wait()
    gather(tok_ref, send_a, None, 0, 4)
    pl.semaphore_wait(barrier, NE - 1 + ND - 1)
    start_part(0, 0, send_a, recv_a)
    gather(tok_ref, send_a, None, 4, ND)
    send_a[ND] = fold[...].astype(BF16)
    start_part(0, 1, send_a, recv_a)
    each(1, NY, lambda k: weight(0, k).start())
    weight_mate0(0).start()
    each(1, NY, lambda k: weight(1, k).start())
    weight_mate0(1).start()
    grad_in.wait()
    gather(grad_ref, send_b, scale, 0, ND)
    send_b[ND] = (fold[...] * scale9).astype(BF16)
    start_wave(1, send_b, recv_b)

    def pass_on(i):
        def body(k):
            weight(i, k).wait_recv()
            weight_mate(i, k).start()
        each(1, NY, body)

    pass_on(0)

    def unfold(buf):
        tail = buf[ND, 0:NS, :]

        def body(c):
            sel = as_bf16(iota((NE, NS), 1) == iota((NE, NS), 0) * 8 + c)
            buf[c, NS:R, :] = dot(sel, tail).astype(BF16)
        each(0, ND, body)

    landed_wave(0, send_a, recv_a)
    unfold(recv_a)
    slice_own(0).start()
    each(1, ND, lambda k: slices(0, k).start())

    weight_own(0).wait()
    weight_mate0(0).wait_recv()
    each(1, NY, lambda k: weight_mate(0, k).wait_recv())

    def contract(dst, rows, mat):
        dst[...] = jnp.zeros_like(dst)

        def body(c):
            dst[...] += dot(rows[c], mat[c])
        each(0, ND, body)

    contract(acc, recv_a, wup)
    hall[dp] = gelu(acc[...]).astype(BF16)
    each(1, ND, lambda k: acts(0, k).start())
    pass_on(1)
    weight_own(1).wait()
    weight_mate0(1).wait_recv()
    each(1, NY, lambda k: weight_mate(1, k).wait_recv())

    def expand(rows, mat, dst):
        fold[...] = jnp.zeros_like(fold)

        def body(c):
            o = dot_cols(rows, mat[c]).astype(BF16)
            dst[c] = o[0:NS]
            put = as_bf16(iota((NS, NE), 0) == iota((NS, NE), 1) * 8 + c)
            fold[...] += dot(put, o[NS:R])
        each(0, ND, body)
        dst[ND] = fold[...].astype(BF16)

    sent_wave(0, send_a, recv_a)
    expand(hall[dp], wdown, send_a)
    start_wave(2, send_a, back_a)

    landed_wave(1, send_b, recv_b)
    unfold(recv_b)
    slice_own(1).start()
    each(1, ND, lambda k: slices(1, k).start())
    contract(acc2, recv_b, wdown)
    pall[dp] = (acc2[...] * gelu_slope(acc[...])).astype(BF16)
    each(1, ND, lambda k: acts(1, k).start())
    sent_wave(1, send_b, recv_b)
    expand(pall[dp], wup, send_b)
    start_wave(3, send_b, back_b)

    def weight_grad(i, act, rows, dst):
        other = (hall, pall)[act]
        slice_own(i).wait()
        each(1, ND, lambda k: slices(i, k).wait_recv())
        each(1, ND, lambda k: acts(act, k).wait_recv())
        wacc[...] = jnp.zeros_like(wacc)

        def body(j):
            wacc[...] += dot_rows(rows[j], other[j])
        each(0, ND, body)
        dst[0] = wacc[...].astype(BF16)

    weight_grad(1, 0, gall, gdown_ref)
    weight_grad(0, 1, xall, gup_ref)

    columns = in_columns(e0.astype(F32), e1.astype(F32), b0.astype(F32), b1.astype(F32), w0, w1)
    f0, f1, r0, r1 = [col.astype(I32) for col in columns[:4]]
    v0, v1 = columns[4:]
    t_iota = iota((T, NS), 1)
    q0 = as_bf16((t_iota == f0 * 8 + r0) & (r0 < 8))
    q1 = as_bf16((t_iota == f1 * 8 + r1) & (r1 < 8))
    landed_wave(2, send_a, back_a)

    def mix(c):
        k0 = as_bf16((t_iota == f0 * 8 + c) & (r0 == 8))
        k1 = as_bf16((t_iota == f1 * 8 + c) & (r1 == 8))
        main, tail = back_a[c], back_a[ND]
        first = dot(q0, main) + dot(k0, tail)
        second = dot(q1, main) + dot(k1, tail)
        out_ref[:, cols(c)] = (first * v0 + second * v1).astype(BF16)
    each(0, ND, mix)

    qs = q0 + q1

    def mix_grad(c):
        ks = as_bf16(((t_iota == f0 * 8 + c) & (r0 == 8)) | ((t_iota == f1 * 8 + c) & (r1 == 8)))
        gtok_ref[:, cols(c)] = (dot(qs, back_b[c]) + dot(ks, back_b[ND])).astype(BF16)

    landed_part(3, 0, send_b, back_b)
    each(3, ND, mix_grad)
    landed_part(3, 1, send_b, back_b)
    each(0, 3, mix_grad)

    sent_wave(2, send_a, back_a)
    sent_wave(3, send_b, back_b)
    for i in (0, 1):
        each(1, NY, lambda k: weight(i, k).wait_send())
        weight_mate0(i).wait_send()
        each(1, NY, lambda k: weight_mate(i, k).wait_send())
        each(1, ND, lambda k: slices(i, k).wait_send())
        each(1, ND, lambda k: acts(i, k).wait_send())


def hand_on_kernel(*refs):
    n = len(refs) // 2
    src, dst, sem = refs[:n], refs[n:2 * n], refs[2 * n]
    out = [pltpu.make_async_copy(src[i], dst[i], sem.at[i]) for i in range(n)]
    for c in out:
        c.start()
    for c in out:
        c.wait()


def hand_on(*arrays):
    n = len(arrays)
    return pl.pallas_call(
        hand_on_kernel,
        name="hand_on",
        out_shape=tuple(jax.ShapeDtypeStruct(a.shape, a.dtype) for a in arrays),
        in_specs=[pl.BlockSpec(memory_space=pltpu.VMEM)] * n,
        out_specs=(pl.BlockSpec(memory_space=pl.ANY),) * n,
        scratch_shapes=[pltpu.SemaphoreType.DMA((n,))],
        compiler_params=pltpu.CompilerParams(vmem_limit_bytes=16000000),
    )(*arrays)


def local(tokens, grad_out, expert_ids, gate_codes, w_up, w_down):
    t, d = tokens.shape
    cw, h = w_up.shape[1], w_up.shape[2]
    ns, r = NE * 8, NE * 9
    vmem = pl.BlockSpec(memory_space=pltpu.VMEM)
    hbm = pl.BlockSpec(memory_space=pl.ANY)
    dma = pltpu.SemaphoreType.DMA
    outs = pl.pallas_call(
        kernel,
        name="moe",
        out_shape=(
            pltpu.VMEM((t, d), BF16), pltpu.VMEM((t, d), BF16),
            pltpu.VMEM((1, cw, h), BF16), pltpu.VMEM((1, cw, h), BF16),
        ),
        in_specs=[hbm] * 2 + [vmem] * 2 + [hbm] * 2,
        out_specs=(vmem,) * 4,
        scratch_shapes=[
            pltpu.VMEM((t, d), BF16), pltpu.VMEM((t, d), BF16),
            pltpu.VMEM((ND + 1, ns, cw), BF16), pltpu.VMEM((ND + 1, ns, cw), BF16),
            pltpu.VMEM((ND + 1, r, cw), BF16), pltpu.VMEM((ND + 1, r, cw), BF16),
            pltpu.VMEM((ND + 1, ns, cw), BF16), pltpu.VMEM((ND + 1, ns, cw), BF16),
            pltpu.VMEM((ND, cw, h), BF16), pltpu.VMEM((ND, cw, h), BF16),
            pltpu.VMEM((ND, r, cw), BF16), pltpu.VMEM((ND, r, cw), BF16),
            pltpu.VMEM((ND, r, h), BF16), pltpu.VMEM((ND, r, h), BF16),
            pltpu.VMEM((r, h), F32), pltpu.VMEM((r, h), F32),
            pltpu.VMEM((ns, cw), F32), pltpu.VMEM((cw, h), F32),
            dma((8 * NE,)), dma((8 * NE,)), dma((2 * NY,)), dma((2 * NY,)),
            dma((2 * NY,)), dma((2 * NY,)), dma((2 * ND,)), dma((2 * ND,)),
            dma((2 * ND,)), dma((2 * ND,)), dma((8,)), dma((16,)),
        ],
        compiler_params=pltpu.CompilerParams(
            collective_id=0, has_side_effects=True, vmem_limit_bytes=62300000),
    )(tokens, grad_out, expert_ids.T, gate_codes.T, w_up, w_down)
    return hand_on(*outs)


def solution(mesh):
    rows = P(("dp", "expert"), None)
    shard = P("expert", "dp", None)
    return jax.shard_map(
        local, mesh=mesh, in_specs=(rows,) * 4 + (shard,) * 2,
        out_specs=(rows, rows, shard, shard), check_vma=False)
```
